32 devices in a mesh: sample: 2 (over y), leaf: 4 (over z), sub: 2 (over x), rhs: 2 (over core).
Axes of the slice: x: 2, y: 2, z: 4, core: 2. Of those that a mesh axis runs over, the one named last changes fastest.
Arguments:
- right_side: float32 [16384, 32], P(('sample', 'leaf', 'sub'), 'rhs'), parts along dimension 0, may hold values from -6 to 6
- leaf_inverse: float32 [64, 256, 256], P(('sample', 'leaf', 'sub')), parts along dimension 0, may hold values from -1 to 2.5
- ubasis: float32 [4, 16384, 128], P(None, ('sample', 'leaf', 'sub'), 'rhs'), parts along dimension 1, may hold values from -6 to 6
- vbasis: float32 [4, 16384, 128], P(None, ('sample', 'leaf', 'sub')), parts along dimension 1, may hold values from -0.00390625 to 0.00390625
Outputs:
- solution: float32 [16384, 32], P(('sample', 'leaf', 'sub'), 'rhs'), parts along dimension 0
The draws below stay inside these ranges and needn't reach their ends.
There are 2 independent parts, one for each index of `sample`. The reference program is written for one: setup_inputs(seed, part) draws one part's arguments, and reference() takes and returns one part's arrays. A program takes and returns all parts, laid end to end along the dimension named above; each array names one. Nothing has to cross between parts.
All inputs are finite; a program needn't handle non-finite values.
Results may differ from the reference program's by a relative error of at most 0.0001.
Values sent between devices are 32-bit elements; how exact they have to be, the bound alone decides.
No kernel may reach another device: no remote copies, remote signals or barrier semaphores. Data moves between devices by JAX's collectives and lax.ppermute only.
A program may use at most 64 MiB of HBM per device.

```python
import jax
import jax.numpy as jnp
from jax import lax

LEAFB = 256
R = 128
NRHS = 32
LEVELS = 4
N = 8192
NLEAF = 32


def draw_leaf_inverse(key, part):
    first_key = jax.random.fold_in(jax.random.fold_in(key, 11), 0)
    eye_block = jnp.eye(LEAFB, dtype=jnp.float32)[None, :, :]
    spread = 0.45 / LEAFB ** 0.5
    noise = jnp.clip(jax.random.normal(first_key, (NLEAF, LEAFB, LEAFB), jnp.float32), -4.0, 4.0)
    return (eye_block + spread * noise).astype(jnp.float32)


def draw_vbasis(key, part):
    level_key = jax.random.fold_in(key, 23)
    child_rows = N / 2.0 ** (jnp.arange(LEVELS).astype(jnp.float32) + 1.0)
    scales = 0.25 / jnp.sqrt(R * child_rows)
    noise = jnp.clip(jax.random.normal(level_key, (LEVELS, N, R), jnp.float32), -4.0, 4.0)
    return (noise * scales[:, None, None]).astype(jnp.float32)


def steps_of(rng, shape, cuts, least, top_value):
    level = 1.0
    for position, parts in cuts:
        steps = jax.random.uniform(jax.random.fold_in(jax.random.fold_in(rng, 6), position), (parts,), jnp.float32, least / len(cuts), top_value / len(cuts))
        level = level * jnp.repeat(jnp.exp(steps), shape[position] // parts).reshape((-1,) + (1,) * (len(shape) - 1 - position))
    return level


def normal_values(key, shape, deviation, limit, pieces=(), kind=jnp.bfloat16):
    array = deviation * jax.random.normal(key, shape, jnp.float32)
    if pieces:
        array = array * steps_of(key, shape, pieces, -0.22, 0.18)
    return jnp.clip(array, -limit, limit).astype(kind)


def setup_inputs(seed: int = 0, part: int = 0) -> dict:
    key_of = jax.random.split(jax.random.key(seed), 5)
    part_keys = jax.random.split(jax.random.fold_in(key_of[4], part), 5)
    right_side = normal_values(part_keys[0], (N, NRHS), 1.0, 6.0, ((0, 8), (1, 2)), jnp.float32)
    leaf_inverse = draw_leaf_inverse(jax.random.fold_in(jax.random.fold_in(key_of[4], part), 71), part)
    ubasis = normal_values(part_keys[2], (LEVELS, N, R), 1.0, 6.0, ((1, 8), (2, 2)), jnp.float32)
    vbasis = draw_vbasis(jax.random.fold_in(jax.random.fold_in(key_of[4], part), 71), part)
    return dict(right_side=right_side, leaf_inverse=leaf_inverse, ubasis=ubasis, vbasis=vbasis)


def pair_flip(values, child_total):
    shaped = values.reshape((child_total // 2, 2) + values.shape[1:])
    return shaped[:, ::-1].reshape(values.shape)

def reference(right_side, leaf_inverse, ubasis, vbasis):
    highest = lax.Precision.HIGHEST
    row_total = right_side.shape[0]
    rhs_count = right_side.shape[1]
    level_total = ubasis.shape[0]
    rank_full = ubasis.shape[2]
    stacked = jnp.concatenate([right_side] + [ubasis[member] for member in range(level_total)], axis=1)
    block_count = leaf_inverse.shape[0]
    block_order = leaf_inverse.shape[1]
    stacked = jnp.einsum('bij,bjw->biw', leaf_inverse, stacked.reshape(block_count, block_order, -1), precision=highest).reshape(row_total, -1)
    for level_now in range(level_total, 0, -1):
        width_now = rhs_count + (level_now - 1) * rank_full
        child_total = 2 ** level_now
        child_rows = row_total // child_total
        own_basis = stacked[:, width_now:width_now + rank_full].reshape(child_total, child_rows, rank_full)
        targets = stacked[:, :width_now].reshape(child_total, child_rows, width_now)
        right_basis = vbasis[level_now - 1].reshape(child_total, child_rows, rank_full)
        gram = jnp.einsum('cnr,cns->crs', right_basis, own_basis, precision=highest)
        proj = jnp.einsum('cnr,cnw->crw', right_basis, targets, precision=highest)
        gram_sib = pair_flip(gram, child_total)
        proj_sib = pair_flip(proj, child_total)
        system = jnp.eye(rank_full, dtype=jnp.float32) - jnp.einsum('crs,cst->crt', gram_sib, gram, precision=highest)
        source = proj_sib - jnp.einsum('crs,csw->crw', gram_sib, proj, precision=highest)
        coeff = jnp.linalg.solve(system, source)
        targets = targets - jnp.einsum('cnr,crw->cnw', own_basis, coeff, precision=highest)
        stacked = jnp.concatenate([targets.reshape(row_total, width_now), stacked[:, width_now:]], axis=1)
    return stacked[:, :rhs_count]
```

```python
import functools

import jax
import jax.numpy as jnp
from jax import lax
from jax.experimental import pallas as pl
from jax.experimental.pallas import tpu as pltpu
from jax.sharding import PartitionSpec as P

F32 = jnp.float32
BF16 = jnp.bfloat16
HIGHEST = lax.Precision.HIGHEST
GRANT = 24 * 1024 * 1024
CLOSE = 1e-12


def dot(left, right):
    return lax.dot_general(left, right, (((1,), (0,)), ((), ())), preferred_element_type=F32)


def dot_full(left, right):
    return lax.dot_general(
        left, right, (((1,), (0,)), ((), ())), precision=HIGHEST, preferred_element_type=F32
    )


def dot_rows(left, right):
    return lax.dot_general(left, right, (((1,), (1,)), ((), ())), preferred_element_type=F32)


def split(value):
    high = value.astype(BF16)
    return high, (value - high.astype(F32)).astype(BF16)


def mul(left, right):
    lh, ll = split(left)
    rh, rl = split(right)
    return dot(lh, rh) + (dot(ll, rh) + dot(lh, rl))


def mul_square(left, right):
    size = right.shape[0]
    lh, ll = split(left)
    rh, rl = split(right)
    weights = jnp.concatenate(
        [
            jnp.concatenate([rh, rl], axis=1),
            jnp.concatenate([rh, jnp.zeros_like(rl)], axis=1),
        ],
        axis=0,
    )
    both = dot(jnp.concatenate([lh, ll], axis=1), weights)
    return both[:, :size] + both[:, size:]


def solve_fast(mine, other, rank):
    other_gram = other[:rank]
    first = mul_square(mine, other_gram)
    power = first[:rank]
    rows = other[rank:] - first[rank:]
    for _ in range(3):
        step = mul_square(jnp.concatenate([power, rows], axis=0), power)
        power = step[:rank]
        rows = rows + step[rank:]
    return rows, jnp.sum(power * power)


def solve_any(mine, other, inverse_ref, rank):
    other_gram = other[:rank]
    first = dot_full(mine, other_gram)
    row_id = lax.broadcasted_iota(jnp.int32, (rank, rank), 0)
    col_id = lax.broadcasted_iota(jnp.int32, (rank, rank), 1)
    eye = jnp.where(row_id == col_id, 1.0, 0.0).astype(F32)
    system = eye - first[:rank]
    source = other[rank:] - first[rank:]
    size = jnp.abs(system)
    scale = jnp.max(jnp.sum(size, axis=0)) * jnp.max(jnp.sum(size, axis=1))
    inverse_ref[...] = system.T / scale

    def unfinished(carry):
        count, error = carry
        return jnp.logical_and(count < 64, jnp.logical_not(error <= CLOSE))

    def improve(carry):
        count, _ = carry
        guess = inverse_ref[...]
        left = eye - dot_full(system, guess)
        inverse_ref[...] = guess + dot_full(guess, left)
        return count + 1, jnp.sum(left * left)

    lax.while_loop(unfinished, improve, (jnp.int32(0), F32(1.0)))
    inverse = inverse_ref[...]
    rows = dot_full(source, inverse)
    return rows + dot_full(source - dot_full(rows, system), inverse)


def solve_pair(mine, other, mine_out, other_out, inverse_ref, rank):
    mine_rows, mine_left = solve_fast(mine(), other(), rank)
    other_rows, other_left = solve_fast(other(), mine(), rank)
    mine_out(mine_rows)
    other_out(other_rows)
    settled = jnp.logical_and(mine_left <= CLOSE, other_left <= CLOSE)

    @pl.when(jnp.logical_not(settled))
    def _():
        mine_out(solve_any(mine(), other(), inverse_ref, rank))
        other_out(solve_any(other(), mine(), inverse_ref, rank))


def store(ref, *index):
    def put(value):
        ref[index if index else ...] = value

    return put


def params(**more):
    return pltpu.CompilerParams(vmem_limit_bytes=GRANT, **more)


def cost(flops, moved):
    return pl.CostEstimate(flops=int(flops), bytes_accessed=int(moved), transcendentals=0)


def turn_body(u_ref, b_ref, ut_ref, bt_ref):
    levels, _, half = u_ref.shape
    for slot in range(levels):
        ut_ref[slot * half : (slot + 1) * half, :] = u_ref[levels - 1 - slot].T
    bt_ref[...] = b_ref[...].T


def turn(ubasis, right_side, blocks):
    levels, rows, half = ubasis.shape
    width = right_side.shape[1]
    step = rows // blocks
    return pl.pallas_call(
        turn_body,
        grid=(blocks,),
        in_specs=[
            pl.BlockSpec((levels, step, half), lambda b: (0, b, 0)),
            pl.BlockSpec((step, width), lambda b: (b, 0)),
        ],
        out_specs=[
            pl.BlockSpec((levels * half, step), lambda b: (0, b)),
            pl.BlockSpec((width, step), lambda b: (0, b)),
        ],
        out_shape=[
            jax.ShapeDtypeStruct((levels * half, rows), F32),
            jax.ShapeDtypeStruct((width, rows), F32),
        ],
        compiler_params=params(),
        cost_estimate=cost(0, 4 * rows * levels * half * 3),
        name="turn",
    )(ubasis, right_side)


def weigh_body(l_ref, v_ref, wh_ref, wl_ref):
    levels, _, rank = v_ref.shape
    turned = l_ref[0].T
    for slot in range(levels):
        product = mul(turned, v_ref[levels - 1 - slot])
        high, low = split(product)
        wh_ref[:, slot * rank : (slot + 1) * rank] = high
        wl_ref[:, slot * rank : (slot + 1) * rank] = low


def weigh(leaf_inverse, vbasis):
    blocks, order, _ = leaf_inverse.shape
    levels, rows, rank = vbasis.shape
    halves = jax.ShapeDtypeStruct((rows, levels * rank), BF16)
    return pl.pallas_call(
        weigh_body,
        grid=(blocks,),
        in_specs=[
            pl.BlockSpec((1, order, order), lambda b: (b, 0, 0)),
            pl.BlockSpec((levels, order, rank), lambda b: (0, b, 0)),
        ],
        out_specs=[pl.BlockSpec((order, levels * rank), lambda b: (b, 0))] * 2,
        out_shape=[halves, halves],
        compiler_params=params(),
        cost_estimate=cost(6 * rows * order * levels * rank, 8 * rows * levels * rank),
        name="weigh",
    )(leaf_inverse, vbasis)


def gather_columns(place, own_ref, other_ref, bt_ref, sh_ref, sl_ref, levels, half):
    for slot in range(levels):
        for source, first in ((own_ref, place), (other_ref, 1 - place)):
            high, low = split(source[slot * half : (slot + 1) * half, :])
            where = pl.ds(pl.multiple_of(slot * 2 * half + first * half, half), half)
            sh_ref[where, :] = high
            sl_ref[where, :] = low
    high, low = split(bt_ref[...])
    sh_ref[levels * 2 * half :, :] = high
    sl_ref[levels * 2 * half :, :] = low


def product_body(children, local, levels, half, place_ref, own_ref, other_ref, bt_ref, wh_ref, wl_ref, *rest):
    rank = 2 * half
    child = pl.program_id(0)
    sh_ref, sl_ref, m_ref, inverse_ref = rest[-4:]
    gather_columns(place_ref[0], own_ref, other_ref, bt_ref, sh_ref, sl_ref, levels, half)
    sh, sl, wh, wl = sh_ref[...], sl_ref[...], wh_ref[...], wl_ref[...]
    m_ref[child] = dot(sh, wh) + (dot(sl, wh) + dot(sh, wl))

    @pl.when(child == children - 1)
    def _():
        taken = wh_ref.shape[1] // rank
        if local == "none":
            for slot in range(taken):
                rest[slot][...] = m_ref[0, :, slot * rank : (slot + 1) * rank]
            return
        if local == "solve":
            coeff_ref = rest[taken - 1]
            solve_pair(
                lambda: m_ref[0, :, :rank],
                lambda: m_ref[1, :, :rank],
                store(coeff_ref, 0),
                store(coeff_ref, 1),
                inverse_ref,
                rank,
            )
            kept, outs = range(1, taken), rest[: taken - 1]
        else:
            coeff_ref = rest[0]
            kept, outs = range(taken), rest[1 : taken + 1]
        coeff = jnp.concatenate([coeff_ref[0], coeff_ref[1]], axis=1)
        for slot, out in zip(kept, outs):
            lanes = slice(slot * rank, (slot + 1) * rank)
            grams = jnp.concatenate([m_ref[0, :rank, lanes], m_ref[1, :rank, lanes]], axis=0)
            out[...] = (m_ref[0, rank:, lanes] + m_ref[1, rank:, lanes]) - mul(coeff, grams)


def product(place, own, other, bt, wh, wl, levels, group, groups, children, coeff=None):
    rows = own.shape[1]
    width = bt.shape[0]
    taken_lanes = wh.shape[1] // groups
    half = own.shape[0] // levels
    rank = 2 * half
    taken = taken_lanes // rank
    step = rows // children
    full = levels * rank + width
    if children == 1:
        local = "none"
        outs = [jax.ShapeDtypeStruct((full, rank), F32)] * taken
    elif coeff is None:
        local = "solve"
        outs = [jax.ShapeDtypeStruct((full - rank, rank), F32)] * (taken - 1)
        outs.append(jax.ShapeDtypeStruct((children, full - rank, rank), F32))
    else:
        local = "apply"
        outs = [jax.ShapeDtypeStruct((full - rank, rank), F32)] * taken
    whole = lambda shape: pl.BlockSpec(shape, lambda c: (0,) * len(shape))
    in_specs = [
        pl.BlockSpec(memory_space=pltpu.SMEM),
        pl.BlockSpec((levels * half, step), lambda c: (0, c)),
        pl.BlockSpec((levels * half, step), lambda c: (0, c)),
        pl.BlockSpec((width, step), lambda c: (0, c)),
        pl.BlockSpec((step, taken_lanes), lambda c: (c, group)),
        pl.BlockSpec((step, taken_lanes), lambda c: (c, group)),
    ]
    args = [place, own, other, bt, wh, wl]
    if local == "apply":
        in_specs.append(whole(coeff.shape))
        args.append(coeff)
    return pl.pallas_call(
        functools.partial(product_body, children, local, levels, half),
        grid=(children,),
        in_specs=in_specs,
        out_specs=[whole(out.shape) for out in outs],
        out_shape=outs,
        scratch_shapes=[
            pltpu.VMEM((full, step), BF16),
            pltpu.VMEM((full, step), BF16),
            pltpu.VMEM((children, full, taken_lanes), F32),
            pltpu.VMEM((rank, rank), F32),
        ],
        compiler_params=params(),
        cost_estimate=cost(6 * rows * full * taken_lanes, 8 * rows * levels * rank),
        name="product",
    )(*args)


def level_body(rank, mine_ref, other_ref, mine_out, other_out, inverse_ref):
    solve_pair(
        lambda: mine_ref[...],
        lambda: other_ref[...],
        store(mine_out),
        store(other_out),
        inverse_ref,
        rank,
    )


def level(mine, other, rank):
    rows = mine.shape[0] - rank
    shape = jax.ShapeDtypeStruct((rows, rank), F32)
    return pl.pallas_call(
        functools.partial(level_body, rank),
        out_shape=[shape, shape],
        scratch_shapes=[pltpu.VMEM((rank, rank), F32)],
        compiler_params=params(),
        cost_estimate=cost(64 * rows * rank * rank, 16 * rows * rank),
        name="level",
    )(mine, other)


def update_body(rank, mine_ref, other_ref, mine_c, other_c, out_ref):
    coeff = jnp.concatenate([mine_c[...], other_c[...]], axis=1)
    grams = jnp.concatenate([mine_ref[:rank, :], other_ref[:rank, :]], axis=0)
    out_ref[...] = (mine_ref[rank:, :] + other_ref[rank:, :]) - mul(coeff, grams)


def update(mine, other, mine_c, other_c, rank):
    rows = mine.shape[0] - rank
    return pl.pallas_call(
        functools.partial(update_body, rank),
        out_shape=jax.ShapeDtypeStruct((rows, rank), F32),
        compiler_params=params(),
        cost_estimate=cost(12 * rows * rank * rank, 20 * rows * rank),
        name="update",
    )(mine, other, mine_c, other_c)


def apply_body(levels, half, children, place_ref, own_ref, other_ref, bt_ref, l_ref, *rest):
    rank = 2 * half
    coeffs = rest[: levels - 1]
    out_ref, sh_ref, sl_ref = rest[levels - 1 :]
    gather_columns(place_ref[0], own_ref, other_ref, bt_ref, sh_ref, sl_ref, levels, half)
    width = bt_ref.shape[0]
    kept = rank + width
    base = (levels - 1) * rank
    blocks, order, _ = l_ref.shape
    shared = {}

    def compose(now, coeff):
        total = coeff[coeff.shape[0] - kept :, :]
        for below in range(2, now):
            first = (now - 1 - below) * rank
            total = total - mul(shared[below], coeff[first : first + rank, :])
        return total

    for now in range(2, levels):
        shared[now] = compose(now, coeffs[levels - now][...])
    top = [
        compose(levels, coeffs[0][child] if children > 1 else coeffs[0][...])
        for child in range(children)
    ]
    lower = [shared[now] for now in range(levels - 1, 1, -1)]
    for block in range(blocks):
        lanes = slice(block * order, (block + 1) * order)
        child = block * children // blocks
        eh, el = split(jnp.concatenate([top[child]] + lower, axis=1))
        uh, ul = sh_ref[:base, lanes], sl_ref[:base, lanes]
        left = (
            sh_ref[base:, lanes].astype(F32)
            + sl_ref[base:, lanes].astype(F32)
            - (dot(eh, uh) + (dot(el, uh) + dot(eh, ul)))
        )
        rh, rl = split(left)
        lh, ll = split(l_ref[block])
        out_ref[:, lanes] = dot_rows(rh, lh) + (dot_rows(rl, lh) + dot_rows(rh, ll))


def apply(place, own, other, bt, leaf_inverse, coeffs, levels, children):
    half = own.shape[0] // levels
    rank = 2 * half
    rows = own.shape[1]
    width = bt.shape[0]
    full = levels * rank + width
    vmem = pl.BlockSpec(memory_space=pltpu.VMEM)
    return pl.pallas_call(
        functools.partial(apply_body, levels, half, children),
        in_specs=[pl.BlockSpec(memory_space=pltpu.SMEM)] + [vmem] * (4 + len(coeffs)),
        out_specs=vmem,
        out_shape=jax.ShapeDtypeStruct((rank + width, rows), F32),
        scratch_shapes=[pltpu.VMEM((full, rows), BF16), pltpu.VMEM((full, rows), BF16)],
        compiler_params=params(),
        cost_estimate=cost(6 * rows * full * (rank + width), 12 * rows * full),
        name="apply",
    )(place, own, other, bt, leaf_inverse, *coeffs)


def root_body(rank, mine_ref, other_ref, rows_ref, out_ref, coeff_ref, inverse_ref):
    coeff, left = solve_fast(mine_ref[...], other_ref[...], rank)
    coeff_ref[...] = coeff

    @pl.when(jnp.logical_not(left <= CLOSE))
    def _():
        coeff_ref[...] = solve_any(mine_ref[...], other_ref[...], inverse_ref, rank)

    out_ref[...] = (rows_ref[rank:, :] - mul(coeff_ref[...], rows_ref[:rank, :])).T


def root(mine, other, rows, rank):
    width = rows.shape[0] - rank
    return pl.pallas_call(
        functools.partial(root_body, rank),
        out_shape=jax.ShapeDtypeStruct((rows.shape[1], width), F32),
        scratch_shapes=[pltpu.VMEM((width, rank), F32), pltpu.VMEM((rank, rank), F32)],
        compiler_params=params(),
        cost_estimate=cost(64 * rank * rank * rank, 8 * rows.shape[0] * rows.shape[1]),
        name="root",
    )(mine, other, rows)


def partner(block, axes, stride):
    count = lax.axis_size(axes)
    return lax.ppermute(block, axes, [(low, low ^ stride) for low in range(count)])


def on_device(right_side, leaf_inverse, ubasis, vbasis):
    levels, rows, half = ubasis.shape
    rank = vbasis.shape[2]
    blocks = leaf_inverse.shape[0]
    tree = ("leaf", "sub")
    devices_all = lax.axis_size(tree)
    children = max(1, 2**levels // devices_all)
    groups = 2
    place = lax.axis_index("rhs").astype(jnp.int32).reshape(1)

    own, bt = turn(ubasis, right_side, blocks)
    other = partner(own, "rhs", 1)
    wh, wl = weigh(leaf_inverse, vbasis)
    upper = product(place, own, other, bt, wh, wl, levels, 0, groups, children)
    coeffs = []
    if children > 1:
        coeffs.append(upper[-1])
        lower = product(place, own, other, bt, wh, wl, levels, 1, groups, children, upper[-1])
        blocks_now = list(upper[:-1]) + list(lower)
        level_now = levels - 1
    else:
        lower = product(place, own, other, bt, wh, wl, levels, 1, groups, children)
        blocks_now = list(upper) + list(lower)
        level_now = levels
    span = devices_all // 2**level_now
    stride = 1
    while stride < span:
        blocks_now = [block + partner(block, tree, stride) for block in blocks_now]
        stride *= 2
    while level_now > 1:
        others = [partner(block, tree, stride) for block in blocks_now]
        mine_c, other_c = level(blocks_now[0], others[0], rank)
        coeffs.append(mine_c)
        blocks_now = [
            update(mine, far, mine_c, other_c, rank)
            for mine, far in zip(blocks_now[1:], others[1:])
        ]
        stride *= 2
        level_now -= 1
    far = partner(blocks_now[0], tree, stride)
    kept = apply(place, own, other, bt, leaf_inverse, coeffs, levels, children)
    return root(blocks_now[0], far, kept, rank)


def solution(mesh):
    placed = (
        P(("sample", "leaf", "sub"), "rhs"),
        P(("sample", "leaf", "sub"), None, None),
        P(None, ("sample", "leaf", "sub"), "rhs"),
        P(None, ("sample", "leaf", "sub"), None),
    )
    return jax.shard_map(
        on_device,
        mesh=mesh,
        in_specs=placed,
        out_specs=P(("sample", "leaf", "sub"), "rhs"),
        check_vma=False,
    )
```

```python
import functools

import jax
import jax.numpy as jnp
from jax import lax
from jax.experimental import pallas as pl
from jax.experimental.pallas import tpu as pltpu
from jax.sharding import PartitionSpec as P

F32 = jnp.float32
BF16 = jnp.bfloat16
HIGHEST = lax.Precision.HIGHEST
GRANT = 24 * 1024 * 1024
CLOSE = 1e-12


def dot(left, right):
    return lax.dot_general(left, right, (((1,), (0,)), ((), ())), preferred_element_type=F32)


def dot_full(left, right):
    return lax.dot_general(
        left, right, (((1,), (0,)), ((), ())), precision=HIGHEST, preferred_element_type=F32
    )


def dot_rows(left, right):
    return lax.dot_general(left, right, (((1,), (1,)), ((), ())), preferred_element_type=F32)


def split(value):
    high = value.astype(BF16)
    return high, (value - high.astype(F32)).astype(BF16)


def mul(left, right):
    lh, ll = split(left)
    rh, rl = split(right)
    return dot(lh, rh) + (dot(ll, rh) + dot(lh, rl))


def mul_square(left, right):
    size = right.shape[0]
    lh, ll = split(left)
    rh, rl = split(right)
    weights = jnp.concatenate(
        [
            jnp.concatenate([rh, rl], axis=1),
            jnp.concatenate([rh, jnp.zeros_like(rl)], axis=1),
        ],
        axis=0,
    )
    both = dot(jnp.concatenate([lh, ll], axis=1), weights)
    return both[:, :size] + both[:, size:]


def solve_fast(mine, other, rank):
    other_gram = other[:rank]
    first = mul_square(mine, other_gram)
    power = first[:rank]
    rows = other[rank:] - first[rank:]
    for _ in range(3):
        step = mul_square(jnp.concatenate([power, rows], axis=0), power)
        power = step[:rank]
        rows = rows + step[rank:]
    return rows, jnp.sum(power * power)


def solve_any(mine, other, inverse_ref, rank):
    other_gram = other[:rank]
    first = dot_full(mine, other_gram)
    row_id = lax.broadcasted_iota(jnp.int32, (rank, rank), 0)
    col_id = lax.broadcasted_iota(jnp.int32, (rank, rank), 1)
    eye = jnp.where(row_id == col_id, 1.0, 0.0).astype(F32)
    system = eye - first[:rank]
    source = other[rank:] - first[rank:]
    size = jnp.abs(system)
    scale = jnp.max(jnp.sum(size, axis=0)) * jnp.max(jnp.sum(size, axis=1))
    inverse_ref[...] = system.T / scale

    def unfinished(carry):
        count, error = carry
        return jnp.logical_and(count < 64, jnp.logical_not(error <= CLOSE))

    def improve(carry):
        count, _ = carry
        guess = inverse_ref[...]
        left = eye - dot_full(system, guess)
        inverse_ref[...] = guess + dot_full(guess, left)
        return count + 1, jnp.sum(left * left)

    lax.while_loop(unfinished, improve, (jnp.int32(0), F32(1.0)))
    inverse = inverse_ref[...]
    rows = dot_full(source, inverse)
    return rows + dot_full(source - dot_full(rows, system), inverse)


def solve_pair(mine, other, mine_out, other_out, inverse_ref, rank):
    mine_rows, mine_left = solve_fast(mine(), other(), rank)
    other_rows, other_left = solve_fast(other(), mine(), rank)
    mine_out(mine_rows)
    other_out(other_rows)
    settled = jnp.logical_and(mine_left <= CLOSE, other_left <= CLOSE)

    @pl.when(jnp.logical_not(settled))
    def _():
        mine_out(solve_any(mine(), other(), inverse_ref, rank))
        other_out(solve_any(other(), mine(), inverse_ref, rank))


def store(ref, *index):
    def put(value):
        ref[index if index else ...] = value

    return put


def in_hbm(array):
    return pltpu.with_memory_space_constraint(array, pltpu.HBM)


def params(**more):
    return pltpu.CompilerParams(vmem_limit_bytes=GRANT, **more)


def cost(flops, moved):
    return pl.CostEstimate(flops=int(flops), bytes_accessed=int(moved), transcendentals=0)


def weigh_body(l_ref, v_ref, wh_ref, wl_ref):
    levels = v_ref.shape[0]
    bases = jnp.concatenate([v_ref[levels - 1 - slot] for slot in range(levels)], axis=1)
    wh_ref[...], wl_ref[...] = split(mul(l_ref[0].T, bases))


def weigh(leaf_inverse, vbasis):
    blocks, order, _ = leaf_inverse.shape
    levels, rows, rank = vbasis.shape
    halves = jax.ShapeDtypeStruct((rows, levels * rank), BF16)
    return pl.pallas_call(
        weigh_body,
        grid=(blocks,),
        in_specs=[
            pl.BlockSpec((1, order, order), lambda b: (b, 0, 0)),
            pl.BlockSpec((levels, order, rank), lambda b: (0, b, 0)),
        ],
        out_specs=[pl.BlockSpec((order, levels * rank), lambda b: (b, 0))] * 2,
        out_shape=[halves, halves],
        compiler_params=params(),
        cost_estimate=cost(6 * rows * order * levels * rank, 8 * rows * levels * rank),
        name="weigh",
    )(in_hbm(leaf_inverse), in_hbm(vbasis))


def gather_columns(place, own_ref, other_ref, bt_ref, sh_ref, sl_ref, levels, half):
    for slot in range(levels):
        for source, first in ((own_ref, place), (other_ref, 1 - place)):
            high, low = split(source[levels - 1 - slot])
            where = pl.ds(pl.multiple_of(slot * 2 * half + first * half, half), half)
            sh_ref[where, :] = high
            sl_ref[where, :] = low
    high, low = split(bt_ref[...])
    sh_ref[levels * 2 * half :, :] = high
    sl_ref[levels * 2 * half :, :] = low


def product_body(children, local, levels, half, place_ref, own_ref, other_ref, bt_ref, wh_ref, wl_ref, *rest):
    rank = 2 * half
    child = pl.program_id(0)
    sh_ref, sl_ref, m_ref, inverse_ref = rest[-4:]
    gather_columns(place_ref[0], own_ref, other_ref, bt_ref, sh_ref, sl_ref, levels, half)
    sh, sl, wh, wl = sh_ref[...], sl_ref[...], wh_ref[...], wl_ref[...]
    m_ref[child] = dot(sh, wh) + (dot(sl, wh) + dot(sh, wl))

    @pl.when(child == children - 1)
    def _():
        taken = wh_ref.shape[1] // rank
        if local == "none":
            for slot in range(taken):
                rest[slot][...] = m_ref[0, :, slot * rank : (slot + 1) * rank]
            return
        if local == "solve":
            coeff_ref = rest[taken - 1]
            solve_pair(
                lambda: m_ref[0, :, :rank],
                lambda: m_ref[1, :, :rank],
                store(coeff_ref, 0),
                store(coeff_ref, 1),
                inverse_ref,
                rank,
            )
            kept, outs = range(1, taken), rest[: taken - 1]
        else:
            coeff_ref = rest[0]
            kept, outs = range(taken), rest[1 : taken + 1]
        coeff = jnp.concatenate([coeff_ref[0], coeff_ref[1]], axis=1)
        for slot, out in zip(kept, outs):
            lanes = slice(slot * rank, (slot + 1) * rank)
            grams = jnp.concatenate([m_ref[0, :rank, lanes], m_ref[1, :rank, lanes]], axis=0)
            out[...] = (m_ref[0, rank:, lanes] + m_ref[1, rank:, lanes]) - mul(coeff, grams)


def product(place, own, other, bt, wh, wl, group, groups, children, coeff=None):
    levels, half, rows = own.shape
    width = bt.shape[0]
    taken_lanes = wh.shape[1] // groups
    rank = 2 * half
    taken = taken_lanes // rank
    step = rows // children
    full = levels * rank + width
    if children == 1:
        local = "none"
        outs = [jax.ShapeDtypeStruct((full, rank), F32)] * taken
    elif coeff is None:
        local = "solve"
        outs = [jax.ShapeDtypeStruct((full - rank, rank), F32)] * (taken - 1)
        outs.append(jax.ShapeDtypeStruct((children, full - rank, rank), F32))
    else:
        local = "apply"
        outs = [jax.ShapeDtypeStruct((full - rank, rank), F32)] * taken
    whole = lambda shape: pl.BlockSpec(shape, lambda c: (0,) * len(shape))
    in_specs = [
        pl.BlockSpec(memory_space=pltpu.SMEM),
        pl.BlockSpec((levels, half, step), lambda c: (0, 0, c)),
        pl.BlockSpec((levels, half, step), lambda c: (0, 0, c)),
        pl.BlockSpec((width, step), lambda c: (0, c)),
        pl.BlockSpec((step, taken_lanes), lambda c: (c, group)),
        pl.BlockSpec((step, taken_lanes), lambda c: (c, group)),
    ]
    args = [place, own, other, bt, wh, wl]
    if local == "apply":
        in_specs.append(whole(coeff.shape))
        args.append(coeff)
    return pl.pallas_call(
        functools.partial(product_body, children, local, levels, half),
        grid=(children,),
        in_specs=in_specs,
        out_specs=[whole(out.shape) for out in outs],
        out_shape=outs,
        scratch_shapes=[
            pltpu.VMEM((full, step), BF16),
            pltpu.VMEM((full, step), BF16),
            pltpu.VMEM((children, full, taken_lanes), F32),
            pltpu.VMEM((rank, rank), F32),
        ],
        compiler_params=params(),
        cost_estimate=cost(6 * rows * full * taken_lanes, 8 * rows * levels * rank),
        name="product",
    )(*args)


def level_body(rank, mine_ref, other_ref, mine_out, other_out, inverse_ref):
    solve_pair(
        lambda: mine_ref[...],
        lambda: other_ref[...],
        store(mine_out),
        store(other_out),
        inverse_ref,
        rank,
    )


def level(mine, other, rank):
    rows = mine.shape[0] - rank
    shape = jax.ShapeDtypeStruct((rows, rank), F32)
    return pl.pallas_call(
        functools.partial(level_body, rank),
        out_shape=[shape, shape],
        scratch_shapes=[pltpu.VMEM((rank, rank), F32)],
        compiler_params=params(),
        cost_estimate=cost(64 * rows * rank * rank, 16 * rows * rank),
        name="level",
    )(mine, other)


def update_body(rank, mine_ref, other_ref, mine_c, other_c, out_ref):
    coeff = jnp.concatenate([mine_c[...], other_c[...]], axis=1)
    grams = jnp.concatenate([mine_ref[:rank, :], other_ref[:rank, :]], axis=0)
    out_ref[...] = (mine_ref[rank:, :] + other_ref[rank:, :]) - mul(coeff, grams)


def update(mine, other, mine_c, other_c, rank):
    rows = mine.shape[0] - rank
    return pl.pallas_call(
        functools.partial(update_body, rank),
        out_shape=jax.ShapeDtypeStruct((rows, rank), F32),
        compiler_params=params(),
        cost_estimate=cost(12 * rows * rank * rank, 20 * rows * rank),
        name="update",
    )(mine, other, mine_c, other_c)


def apply_body(levels, half, children, place_ref, own_ref, other_ref, bt_ref, l_ref, *rest):
    rank = 2 * half
    coeffs = rest[: levels - 1]
    out_ref, sh_ref, sl_ref = rest[levels - 1 :]
    gather_columns(place_ref[0], own_ref, other_ref, bt_ref, sh_ref, sl_ref, levels, half)
    width = bt_ref.shape[0]
    kept = rank + width
    base = (levels - 1) * rank
    blocks, order, _ = l_ref.shape
    shared = {}

    def compose(now, coeff):
        total = coeff[coeff.shape[0] - kept :, :]
        for below in range(2, now):
            first = (now - 1 - below) * rank
            total = total - mul(shared[below], coeff[first : first + rank, :])
        return total

    for now in range(2, levels):
        shared[now] = compose(now, coeffs[levels - now][...])
    top = [
        compose(levels, coeffs[0][child] if children > 1 else coeffs[0][...])
        for child in range(children)
    ]
    lower = [shared[now] for now in range(levels - 1, 1, -1)]
    for block in range(blocks):
        lanes = slice(block * order, (block + 1) * order)
        child = block * children // blocks
        eh, el = split(jnp.concatenate([top[child]] + lower, axis=1))
        uh, ul = sh_ref[:base, lanes], sl_ref[:base, lanes]
        left = (
            sh_ref[base:, lanes].astype(F32)
            + sl_ref[base:, lanes].astype(F32)
            - (dot(eh, uh) + (dot(el, uh) + dot(eh, ul)))
        )
        rh, rl = split(left)
        lh, ll = split(l_ref[block])
        out_ref[:, lanes] = dot_rows(rh, lh) + (dot_rows(rl, lh) + dot_rows(rh, ll))


def apply(place, own, other, bt, leaf_inverse, coeffs, children):
    levels, half, rows = own.shape
    rank = 2 * half
    width = bt.shape[0]
    full = levels * rank + width
    vmem = pl.BlockSpec(memory_space=pltpu.VMEM)
    return pl.pallas_call(
        functools.partial(apply_body, levels, half, children),
        in_specs=[pl.BlockSpec(memory_space=pltpu.SMEM)] + [vmem] * (4 + len(coeffs)),
        out_specs=vmem,
        out_shape=jax.ShapeDtypeStruct((rank + width, rows), F32),
        scratch_shapes=[pltpu.VMEM((full, rows), BF16), pltpu.VMEM((full, rows), BF16)],
        compiler_params=params(),
        cost_estimate=cost(6 * rows * full * (rank + width), 12 * rows * full),
        name="apply",
    )(place, own, other, bt, leaf_inverse, *coeffs)


def root_body(rank, mine_ref, other_ref, rows_ref, out_ref, coeff_ref, inverse_ref):
    coeff, left = solve_fast(mine_ref[...], other_ref[...], rank)
    coeff_ref[...] = coeff

    @pl.when(jnp.logical_not(left <= CLOSE))
    def _():
        coeff_ref[...] = solve_any(mine_ref[...], other_ref[...], inverse_ref, rank)

    out_ref[...] = (rows_ref[rank:, :] - mul(coeff_ref[...], rows_ref[:rank, :]))


def root(mine, other, rows, rank):
    width = rows.shape[0] - rank
    return pl.pallas_call(
        functools.partial(root_body, rank),
        out_shape=jax.ShapeDtypeStruct((width, rows.shape[1]), F32),
        scratch_shapes=[pltpu.VMEM((width, rank), F32), pltpu.VMEM((rank, rank), F32)],
        compiler_params=params(),
        cost_estimate=cost(64 * rank * rank * rank, 8 * rows.shape[0] * rows.shape[1]),
        name="root",
    )(mine, other, rows)


def partner(block, axes, stride):
    count = lax.axis_size(axes)
    return lax.ppermute(block, axes, [(low, low ^ stride) for low in range(count)])


def on_device(right_side, leaf_inverse, ubasis, vbasis):
    levels, rows, half = ubasis.shape
    rank = vbasis.shape[2]
    blocks = leaf_inverse.shape[0]
    tree = ("leaf", "sub")
    devices_all = lax.axis_size(tree)
    children = max(1, 2**levels // devices_all)
    groups = 2
    place = lax.axis_index("rhs").astype(jnp.int32).reshape(1)

    own, bt = jnp.swapaxes(ubasis, 1, 2), right_side.T
    other = partner(own, "rhs", 1)
    wh, wl = weigh(leaf_inverse, vbasis)
    upper = product(place, own, other, bt, wh, wl, 0, groups, children)
    coeffs = []
    if children > 1:
        coeffs.append(upper[-1])
        lower = product(place, own, other, bt, wh, wl, 1, groups, children, upper[-1])
        blocks_now = list(upper[:-1]) + list(lower)
        level_now = levels - 1
    else:
        lower = product(place, own, other, bt, wh, wl, 1, groups, children)
        blocks_now = list(upper) + list(lower)
        level_now = levels
    span = devices_all // 2**level_now
    stride = 1
    while stride < span:
        blocks_now = [block + partner(block, tree, stride) for block in blocks_now]
        stride *= 2
    while level_now > 1:
        others = [partner(block, tree, stride) for block in blocks_now]
        mine_c, other_c = level(blocks_now[0], others[0], rank)
        coeffs.append(mine_c)
        blocks_now = [
            update(mine, far, mine_c, other_c, rank)
            for mine, far in zip(blocks_now[1:], others[1:])
        ]
        stride *= 2
        level_now -= 1
    far = partner(blocks_now[0], tree, stride)
    kept = apply(place, own, other, bt, leaf_inverse, coeffs, children)
    return root(blocks_now[0], far, kept, rank).T


def solution(mesh):
    placed = (
        P(("sample", "leaf", "sub"), "rhs"),
        P(("sample", "leaf", "sub"), None, None),
        P(None, ("sample", "leaf", "sub"), "rhs"),
        P(None, ("sample", "leaf", "sub"), None),
    )
    return jax.shard_map(
        on_device,
        mesh=mesh,
        in_specs=placed,
        out_specs=P(("sample", "leaf", "sub"), "rhs"),
        check_vma=False,
    )
```

```python
import functools

import jax
import jax.numpy as jnp
from jax import lax
from jax.experimental import pallas as pl
from jax.experimental.pallas import tpu as pltpu
from jax.sharding import PartitionSpec as P


F32 = jnp.float32
BF16 = jnp.bfloat16
HIGHEST = lax.Precision.HIGHEST
GRANT = 24 * 1024 * 1024
CLOSE = 1e-11
EXACT = 1e-9
VMEM = pl.BlockSpec(memory_space=pltpu.VMEM)
SMEM = pl.BlockSpec(memory_space=pltpu.SMEM)


def dot(left, right):
    return lax.dot_general(left, right, (((1,), (0,)), ((), ())), preferred_element_type=F32)


def dot_full(left, right):
    return lax.dot_general(
        left, right, (((1,), (0,)), ((), ())), precision=HIGHEST, preferred_element_type=F32
    )


def dot_rows(left, right):
    return lax.dot_general(left, right, (((1,), (1,)), ((), ())), preferred_element_type=F32)


def split(value):
    high = value.astype(BF16)
    return high, (value - high.astype(F32)).astype(BF16)


def mul(left, right):
    return dot_halves(*split(left), *split(right))


def dot_halves(lh, ll, rh, rl):
    return dot(jnp.concatenate([lh, ll, lh], axis=1), jnp.concatenate([rh, rh, rl], axis=0))


def mul_square(left, right):
    size = right.shape[0]
    lh, ll = split(left)
    rh, rl = split(right)
    weights = jnp.concatenate(
        [
            jnp.concatenate([rh, rl], axis=1),
            jnp.concatenate([rh, jnp.zeros_like(rl)], axis=1),
        ],
        axis=0,
    )
    both = dot(jnp.concatenate([lh, ll], axis=1), weights)
    return both[:, :size] + both[:, size:]


def series(mine, other, rank, factors):
    first = mul_square(mine, other[:rank])
    power = first[:rank]
    rows = other[rank:] - first[rank:]
    for _ in range(factors):
        step = mul_square(jnp.concatenate([power, rows], axis=0), power)
        power = step[:rank]
        rows = rows + step[rank:]
    return rows, jnp.sum(power * power)


def solve_any(mine, other, inverse_ref, rank):
    other_gram = other[:rank]
    first = dot_full(mine, other_gram)
    row_id = lax.broadcasted_iota(jnp.int32, (rank, rank), 0)
    col_id = lax.broadcasted_iota(jnp.int32, (rank, rank), 1)
    eye = jnp.where(row_id == col_id, 1.0, 0.0).astype(F32)
    system = eye - first[:rank]
    source = other[rank:] - first[rank:]
    size = jnp.abs(system)
    scale = jnp.max(jnp.sum(size, axis=0)) * jnp.max(jnp.sum(size, axis=1))
    inverse_ref[...] = system.T / scale

    def unfinished(carry):
        count, error = carry
        return jnp.logical_and(count < 64, jnp.logical_not(error <= EXACT))

    def improve(carry):
        count, _ = carry
        guess = inverse_ref[...]
        left = eye - dot_full(system, guess)
        inverse_ref[...] = guess + dot_full(guess, left)
        return count + 1, jnp.sum(left * left)

    lax.while_loop(unfinished, improve, (jnp.int32(0), F32(1.0)))
    inverse = inverse_ref[...]
    rows = dot_full(source, inverse)
    return rows + dot_full(source - dot_full(rows, system), inverse)


def solve(systems, inverse_ref, rank, finish):
    short = [series(mine(), other(), rank, 3) for mine, other, _ in systems]
    finish([rows for rows, _ in short])
    worst = functools.reduce(jnp.maximum, [left for _, left in short])

    @pl.when(jnp.logical_not(worst <= CLOSE))
    def _():
        for mine, other, hold in systems:
            rows, left = series(mine(), other(), rank, 5)
            hold[...] = rows

            @pl.when(jnp.logical_not(left <= CLOSE))
            def _():
                hold[...] = solve_any(mine(), other(), inverse_ref, rank)

        finish([hold[...] for _, _, hold in systems])


def in_hbm(array):
    return pltpu.with_memory_space_constraint(array, pltpu.HBM)


def params(**more):
    return pltpu.CompilerParams(vmem_limit_bytes=GRANT, **more)


def cost(flops, moved):
    return pl.CostEstimate(flops=int(flops), bytes_accessed=int(moved), transcendentals=0)


def weigh_body(l_hbm, v_hbm, wh_ref, wl_ref, l_ref, v_ref, l_sem, v_sem):
    blocks, order, _ = l_ref.shape
    levels = v_ref.shape[0]

    def loads(block):
        rows = pl.ds(block * order, order)
        return (
            pltpu.make_async_copy(l_hbm.at[block], l_ref.at[block], l_sem.at[block]),
            pltpu.make_async_copy(v_hbm.at[:, rows, :], v_ref.at[:, rows, :], v_sem.at[block]),
        )

    for block in range(blocks):
        for load in loads(block):
            load.start()
    for block in range(blocks):
        rows = slice(block * order, (block + 1) * order)
        for load in loads(block):
            load.wait()
        bases = jnp.concatenate([v_ref[levels - 1 - slot, rows, :] for slot in range(levels)], axis=1)
        wh_ref[rows, :], wl_ref[rows, :] = split(mul(l_ref[block].T, bases))


def weigh(leaf_inverse, vbasis):
    blocks, order, _ = leaf_inverse.shape
    levels, rows, rank = vbasis.shape
    halves = jax.ShapeDtypeStruct((rows, levels * rank), BF16)
    return pl.pallas_call(
        weigh_body,
        in_specs=[pl.BlockSpec(memory_space=pltpu.HBM)] * 2,
        out_specs=[VMEM] * 2,
        out_shape=[halves, halves],
        scratch_shapes=[
            pltpu.VMEM(leaf_inverse.shape, F32),
            pltpu.VMEM(vbasis.shape, F32),
            pltpu.SemaphoreType.DMA((blocks,)),
            pltpu.SemaphoreType.DMA((blocks,)),
        ],
        compiler_params=params(),
        cost_estimate=cost(6 * rows * order * levels * rank, 8 * rows * levels * rank),
        name="weigh",
    )(in_hbm(leaf_inverse), in_hbm(vbasis))


def gather_columns(place, own_ref, other_ref, bt_ref, sh_ref, sl_ref, whole):
    levels, half, _ = own_ref.shape
    for slot in range(levels):
        sources = ((own_ref, place), (other_ref, 1 - place)) if slot < whole else ((own_ref, 0),)
        base = slot * 2 * half if slot < whole else (whole + slot) * half
        for source, first in sources:
            high, low = split(source[levels - 1 - slot])
            where = pl.ds(pl.multiple_of(base + first * half, half), half)
            sh_ref[where, :] = high
            sl_ref[where, :] = low
    high, low = split(bt_ref[...])
    sh_ref[(whole + levels) * half :, :] = high
    sl_ref[(whole + levels) * half :, :] = low


def in_order(place, mine, other, half):
    count = mine.shape[0] // half
    pieces = [(mine[n * half : (n + 1) * half], other[n * half : (n + 1) * half]) for n in range(count)]
    return [
        jnp.where(place == 0, jnp.concatenate([a, b], axis=0), jnp.concatenate([b, a], axis=0))
        for a, b in pieces
    ]


def block_of(place_ref, refs, half):
    def read():
        if len(refs) == 1:
            return refs[0][...]
        mine, other = refs[0][...], refs[1][...]
        shared = mine.shape[0] // half * half
        levels = in_order(place_ref[0], mine[:shared], other[:shared], half)
        return jnp.concatenate(levels + [mine[shared:]], axis=0)

    return read


def multiply(sh_ref, sl_ref, wh_ref, wl_ref, child, step, lanes):
    rows = slice(child * step, (child + 1) * step)
    return dot_halves(sh_ref[:, rows], sl_ref[:, rows], wh_ref[rows, lanes], wl_ref[rows, lanes])


def upper_body(children, taken, whole, rank, place_ref, own_ref, other_ref, bt_ref, wh_ref, wl_ref, *rest):
    sh_ref, sl_ref = rest[:2]
    outs = rest[2:]
    step = own_ref.shape[2] // children
    gather_columns(place_ref[0], own_ref, other_ref, bt_ref, sh_ref, sl_ref, whole)
    lanes = slice(0, taken * rank)
    if children == 1:
        whole = multiply(sh_ref, sl_ref, wh_ref, wl_ref, 0, step, lanes)
        for slot in range(taken):
            outs[slot][...] = whole[:, slot * rank : (slot + 1) * rank]
        return
    coeff_ref, m_ref, inverse_ref = outs[taken - 1], outs[-2], outs[-1]
    for child in range(children):
        m_ref[child] = multiply(sh_ref, sl_ref, wh_ref, wl_ref, child, step, lanes)
    first, second = lambda: m_ref[0, :, :rank], lambda: m_ref[1, :, :rank]

    def finish(found):
        coeff_ref[0], coeff_ref[1] = found
        coeff = jnp.concatenate(found, axis=1)
        for slot in range(1, taken):
            local_update(m_ref, slot, rank, coeff, outs[slot - 1])

    systems = ((first, second, coeff_ref.at[0]), (second, first, coeff_ref.at[1]))
    solve(systems, inverse_ref, rank, finish)


def local_update(m_ref, slot, rank, coeff, out):
    lanes = slice(slot * rank, (slot + 1) * rank)
    grams = jnp.concatenate([m_ref[0, :rank, lanes], m_ref[1, :rank, lanes]], axis=0)
    out[...] = (m_ref[0, rank:, lanes] + m_ref[1, rank:, lanes]) - mul(coeff, grams)


def lower_body(children, taken, rank, sh_ref, sl_ref, wh_ref, wl_ref, *rest):
    step = sh_ref.shape[1] // children
    first = wh_ref.shape[1] - taken * rank
    lanes = slice(first, first + taken * rank)
    if children == 1:
        whole = multiply(sh_ref, sl_ref, wh_ref, wl_ref, 0, step, lanes)
        for slot in range(taken):
            rest[slot][...] = whole[:, slot * rank : (slot + 1) * rank]
        return
    coeff_ref, out_ref, *later, m_ref = rest
    for child in range(children):
        product = multiply(sh_ref, sl_ref, wh_ref, wl_ref, child, step, lanes)
        m_ref[child] = product[:, :rank]
        for slot in range(1, taken):
            later[slot - 1][child] = product[:, slot * rank : (slot + 1) * rank]
    settle(m_ref, coeff_ref, out_ref)


def settle(m_ref, coeff_ref, out_ref):
    coeff = jnp.concatenate([coeff_ref[0], coeff_ref[1]], axis=1)
    local_update(m_ref, 0, coeff.shape[1] // 2, coeff, out_ref)


def array(*shape, dtype=F32):
    return jax.ShapeDtypeStruct(shape, dtype)


def upper(place, own, other, bt, wh, wl, taken, whole, children):
    levels, half, rows = own.shape
    rank = 2 * half
    first = (whole + levels) * half + bt.shape[0]
    outs = [array(first, rows, dtype=BF16)] * 2
    scratch = []
    if children > 1:
        outs += [array(first - rank, rank)] * (taken - 1) + [array(children, first - rank, rank)]
        scratch = [pltpu.VMEM((children, first, taken * rank), F32), pltpu.VMEM((rank, rank), F32)]
    else:
        outs += [array(first, rank)] * taken
    return pl.pallas_call(
        functools.partial(upper_body, children, taken, whole, rank),
        in_specs=[SMEM] + [VMEM] * 5,
        out_specs=[VMEM] * len(outs),
        out_shape=outs,
        scratch_shapes=scratch,
        compiler_params=params(),
        cost_estimate=cost(6 * rows * first * taken * rank, 8 * rows * levels * rank),
        name="upper",
    )(place, own, other, bt, wh, wl)


def lower(sh, sl, wh, wl, coeff, rank, taken, children):
    first, rows = sh.shape
    args, scratch = [sh, sl, wh, wl], []
    if children > 1:
        outs = [array(first - rank, rank)] + [array(children, first, rank)] * (taken - 1)
        args.append(coeff)
        scratch = [pltpu.VMEM((children, first, rank), F32)]
    else:
        outs = [array(first, rank)] * taken
    return pl.pallas_call(
        functools.partial(lower_body, children, taken, rank),
        in_specs=[VMEM] * len(args),
        out_specs=[VMEM] * len(outs),
        out_shape=outs,
        scratch_shapes=scratch,
        compiler_params=params(),
        cost_estimate=cost(6 * rows * first * taken * rank, 4 * rows * first),
        name="lower",
    )(*args)


def after_local(made, coeff):
    _, first, rank = made.shape
    return pl.pallas_call(
        settle,
        in_specs=[VMEM, VMEM],
        out_specs=VMEM,
        out_shape=array(first - rank, rank),
        compiler_params=params(),
        cost_estimate=cost(12 * first * rank * rank, 16 * first * rank),
        name="after",
    )(made, coeff)


def level_body(rank, counts, place_ref, *rest):
    near = block_of(place_ref, rest[: counts[0]], rank // 2)
    distant = block_of(place_ref, rest[counts[0] : sum(counts)], rank // 2)
    mine_out, other_out, inverse_ref = rest[sum(counts) :]

    def finish(found):
        mine_out[...], other_out[...] = found

    solve(((near, distant, mine_out), (distant, near, other_out)), inverse_ref, rank, finish)


def block_rows(refs, half):
    rows = refs[0].shape[0]
    return rows + (rows // half * half if len(refs) > 1 else 0)


def level(place, mine, far, rank):
    rows = block_rows(mine, rank // 2) - rank
    return pl.pallas_call(
        functools.partial(level_body, rank, (len(mine), len(far))),
        in_specs=[SMEM] + [VMEM] * (len(mine) + len(far)),
        out_specs=[VMEM] * 2,
        out_shape=[array(rows, rank)] * 2,
        scratch_shapes=[pltpu.VMEM((rank, rank), F32)],
        compiler_params=params(),
        cost_estimate=cost(64 * rows * rank * rank, 16 * rows * rank),
        name="level",
    )(place, *mine, *far)


def update_body(rank, counts, place_ref, *rest):
    near = block_of(place_ref, rest[: counts[0]], rank // 2)()
    distant = block_of(place_ref, rest[counts[0] : sum(counts)], rank // 2)()
    mine_c, other_c, out_ref = rest[sum(counts) :]
    coeff = jnp.concatenate([mine_c[...], other_c[...]], axis=1)
    grams = jnp.concatenate([near[:rank], distant[:rank]], axis=0)
    out_ref[...] = (near[rank:] + distant[rank:]) - mul(coeff, grams)


def update(place, mine, far, mine_c, other_c, rank):
    rows = block_rows(mine, rank // 2) - rank
    return pl.pallas_call(
        functools.partial(update_body, rank, (len(mine), len(far))),
        in_specs=[SMEM] + [VMEM] * (2 + len(mine) + len(far)),
        out_specs=VMEM,
        out_shape=array(rows, rank),
        compiler_params=params(),
        cost_estimate=cost(12 * rows * rank * rank, 20 * rows * rank),
        name="update",
    )(place, *mine, *far, mine_c, other_c)


def pack_body(top_ref, next_ref, out_ref):
    part = out_ref.shape[0] // (top_ref.shape[0] + 1)
    skip = top_ref.shape[1] - next_ref.shape[0]
    for child in range(top_ref.shape[0]):
        out_ref[child * part : (child + 1) * part, :] = top_ref[child, skip : skip + part, :]
    out_ref[top_ref.shape[0] * part :, :] = next_ref[:part, :]


def pack(top, following, width):
    part = following.shape[0] - width
    return pl.pallas_call(
        pack_body,
        in_specs=[VMEM] * 2,
        out_specs=VMEM,
        out_shape=array((top.shape[0] + 1) * part, top.shape[2]),
        compiler_params=params(),
        cost_estimate=cost(0, 8 * (top.shape[0] + 1) * part * top.shape[2]),
        name="pack",
    )(top, following)


def apply_body(children, place_ref, own_ref, other_ref, bt_ref, l_ref, *rest):
    levels, half, _ = own_ref.shape
    rank, width = 2 * half, bt_ref.shape[0]
    coeffs = rest[: levels - 1]
    out_ref, sh_ref, sl_ref = rest[-3:]
    gather_columns(place_ref[0], own_ref, other_ref, bt_ref, sh_ref, sl_ref, levels)
    kept = rank + width
    base = (levels - 1) * rank
    blocks, order, _ = l_ref.shape
    shared = {}

    def compose(now, coeff):
        total = coeff[coeff.shape[0] - kept :, :]
        for below in range(2, now):
            first = (now - 1 - below) * rank
            total = total - mul(shared[below], coeff[first : first + rank, :])
        return total

    def widened(coeff, part):
        count = coeff.shape[0] - width if part == children else part_rows
        mine = coeff[coeff.shape[0] - width - count : coeff.shape[0] - width]
        far = rest[levels - 1][part * part_rows : (part + 1) * part_rows, :]
        kept_rows = coeff[: coeff.shape[0] - width - count]
        pieces = in_order(place_ref[0], mine, far, half)
        return jnp.concatenate([kept_rows] * (kept_rows.shape[0] > 0) + pieces + [coeff[-width:]], axis=0)

    full = [coeff[...] for coeff in coeffs]
    if children > 1:
        part_rows = coeffs[1].shape[0] - width
        full[1] = widened(full[1], children)
        tops = [widened(coeffs[0][child], child) for child in range(children)]
    else:
        tops = [full[0]]
    for now in range(2, levels):
        shared[now] = compose(now, full[levels - now])
    top = [compose(levels, coeff) for coeff in tops]
    lower = [shared[now] for now in range(levels - 1, 1, -1)]
    for block in range(blocks):
        lanes = slice(block * order, (block + 1) * order)
        child = block * children // blocks
        eh, el = split(jnp.concatenate([top[child]] + lower, axis=1))
        uh, ul = sh_ref[:base, lanes], sl_ref[:base, lanes]
        left = (
            sh_ref[base:, lanes].astype(F32)
            + sl_ref[base:, lanes].astype(F32)
            - dot_halves(eh, el, uh, ul)
        )
        rh, rl = split(left)
        lh, ll = split(l_ref[block])
        out_ref[:, lanes] = dot_rows(
            jnp.concatenate([rh, rl, rh], axis=1), jnp.concatenate([lh, lh, ll], axis=1)
        )


def apply(place, own, other, bt, leaf_inverse, coeffs, swapped, children):
    levels, half, rows = own.shape
    rank, width = 2 * half, bt.shape[0]
    full, kept = levels * rank + width, rank + width
    args = [own, other, bt, leaf_inverse, *coeffs] + ([swapped] if children > 1 else [])
    return pl.pallas_call(
        functools.partial(apply_body, children),
        in_specs=[SMEM] + [VMEM] * len(args),
        out_specs=VMEM,
        out_shape=array(kept, rows),
        scratch_shapes=[pltpu.VMEM((full, rows), BF16)] * 2,
        compiler_params=params(),
        cost_estimate=cost(6 * rows * full * kept, 12 * rows * full),
        name="apply",
    )(place, *args)


def root_body(rank, mine_ref, other_ref, rows_ref, out_ref, coeff_ref, inverse_ref):
    def finish(found):
        out_ref[...] = rows_ref[rank:, :] - mul(found[0], rows_ref[:rank, :])

    system = (lambda: mine_ref[...], lambda: other_ref[...], coeff_ref)
    solve((system,), inverse_ref, rank, finish)


def root(mine, other, rows, rank):
    width = rows.shape[0] - rank
    return pl.pallas_call(
        functools.partial(root_body, rank),
        in_specs=[VMEM] * 3,
        out_specs=VMEM,
        out_shape=jax.ShapeDtypeStruct((width, rows.shape[1]), F32),
        scratch_shapes=[pltpu.VMEM((width, rank), F32), pltpu.VMEM((rank, rank), F32)],
        compiler_params=params(),
        cost_estimate=cost(64 * rank * rank * rank, 8 * rows.shape[0] * rows.shape[1]),
        name="root",
    )(mine, other, rows)


def partner(block, axes, stride):
    count = lax.axis_size(axes)
    return lax.ppermute(block, axes, [(low, low ^ stride) for low in range(count)])


def on_device(right_side, leaf_inverse, ubasis, vbasis):
    levels, _, _ = ubasis.shape
    rank, width = vbasis.shape[2], right_side.shape[1]
    tree = ("leaf", "sub")
    devices_all = lax.axis_size(tree)
    children = max(1, 2**levels // devices_all)
    place = lax.axis_index("rhs").astype(jnp.int32).reshape(1)

    own, bt = jnp.swapaxes(ubasis, 1, 2), right_side.T
    other = partner(own, "rhs", 1)
    wh, wl = weigh(leaf_inverse, vbasis)
    taken = levels // 2
    under = levels - taken
    whole = 2 if children > 1 else levels
    sh, sl, *made = upper(place, own, other, bt, wh, wl, taken, whole, children)
    coeffs = []
    level_now = levels
    if children > 1:
        coeffs.append(made.pop())
        level_now -= 1
    more = lower(sh, sl, wh, wl, coeffs[-1] if coeffs else None, rank, under, children)
    near = list(made) + list(more)
    if coeffs:
        for row in range(1, under):
            near[-row] = after_local(near[-row], coeffs[0])
    span = devices_all // 2**level_now
    stride = 1
    while stride < span:
        near = [block + partner(block, tree, stride) for block in near]
        stride *= 2
    halved, swapped = False, None
    while level_now > 1:
        rows_of = range(level_now, 0, -1)
        far = []
        for at, row in enumerate(rows_of):
            got = partner(near[at], tree, stride)
            if halved:
                near[at] = (near[at], partner(near[at], "rhs", 1))
                far.append((got, partner(got, "rhs", 1)))
            else:
                near[at] = (near[at],)
                far.append((got,))
        mine_c, other_c = level(place, near[0], far[0], rank)
        coeffs.append(mine_c)
        made = []
        for row, mine, other_block in zip(rows_of[1:], near[1:], far[1:]):
            made.append(update(place, mine, other_block, mine_c, other_c, rank))
        near = made
        halved = children > 1 and level_now == levels - 1
        if halved:
            swapped = pack(coeffs[0], mine_c, width)
            swapped = partner(swapped, "rhs", 1)
        stride *= 2
        level_now -= 1
    last = partner(near[0], tree, stride)
    kept = apply(place, own, other, bt, leaf_inverse, coeffs, swapped, children)
    return root(near[0], last, kept, rank).T


def solution(mesh):
    placed = (
        P(("sample", "leaf", "sub"), "rhs"),
        P(("sample", "leaf", "sub"), None, None),
        P(None, ("sample", "leaf", "sub"), "rhs"),
        P(None, ("sample", "leaf", "sub"), None),
    )
    return jax.shard_map(
        on_device,
        mesh=mesh,
        in_specs=placed,
        out_specs=P(("sample", "leaf", "sub"), "rhs"),
        check_vma=False,
    )
```
